512 devices in a mesh: blk: 64 (over z_lo, y, core), rows: 8 (over z_hi, x).
Axes of the slice: x: 4, y: 4, z: 16 (z_hi: 2, z_lo: 8; z = z_hi * 8 + z_lo), core: 2. Of those that a mesh axis runs over, the one named last changes fastest.
Arguments:
- q_panel: bfloat16 [8, 2048, 256], P('rows', 'blk'), may hold values from -6 to 6
- tiles: bfloat16 [64, 8, 80, 128, 128], P('blk', 'rows'), may hold values from -0.078125 to 0.078125
- tile_rows: int32 [64, 8, 80], P('blk', 'rows'), may hold values from 0 to 15
- tile_cols: int32 [64, 8, 80, 1], P('blk', 'rows'), may hold values from 0 to 15; in each aligned block of 80 rows (0 to 79, 80 to 159, ..., all dimensions but the last counted through in order) at most 7 rows name the same one
- tile_count: int32 [64, 8], P('blk', 'rows'), may hold values from 40 to 80, as said below
- owner_map: int32 [64, 16], P('blk'), may hold values from 0 to 15, each once within a row
Outputs:
- y_basis: bfloat16 [64, 2048, 256], P('blk', 'rows')
- z_basis: float32 [8, 2048, 256], P('rows', 'blk')
The draws below stay inside these ranges and needn't reach their ends.
Inputs may be any that keep to these rules, and one draw needn't show every extreme that they name: The live tiles of a device are its first tile_count slots; some device has all 80 live and some has 40. `tile_cols`: among the 80 slots of one device no column block appears more than 7 times. Each row of owner_map is a permutation; slot s belongs to the device with rows index s // 2.
All inputs are finite; a program needn't handle non-finite values.
Results may differ from the reference program's by a relative error of at most 0.0013.
Values may be sent and summed in bfloat16 or wider, within the bound.
A program may use at most 64 MiB of HBM per device.

```python
import math
import jax
import jax.numpy as jnp
import numpy as np
from jax import lax

TILE = 128
RANK = 256
TPB = 5
RB_DEV = 2
MOST = 7
NCB = 16
TILES_DEV = 80
RBG = 16
N_BLK = 64
N_ROWS = 8


def draw_tile_count(key, part):
    counts = jax.random.randint(key, (N_BLK * N_ROWS,), TILES_DEV // 2, TILES_DEV + 1)
    picked = jax.random.permutation(jax.random.fold_in(key, 7), N_BLK * N_ROWS)
    counts = counts.at[picked[0]].set(TILES_DEV).at[picked[1]].set(TILES_DEV // 2)
    return counts.reshape(N_BLK, N_ROWS).astype(jnp.int32)


def with_ends(entries, stream_key, low, largest):
    shape = entries.shape
    spot = [jax.random.randint(jax.random.fold_in(stream_key, axis), (), 0, shape[axis]) for axis in range(len(shape))]
    entries = entries.at[tuple(spot)].set(low)
    longest = shape.index(max(shape))
    spot[longest] = (spot[longest] + 1) % shape[longest]
    return entries.at[tuple(spot)].set(largest)


def block_levels(stream_key, dims, split, smallest, top_value):
    factor_of = 1.0
    for position, parts in split:
        draws = jax.random.uniform(jax.random.fold_in(jax.random.fold_in(stream_key, 6), position), (parts,), jnp.float32, smallest / len(split), top_value / len(split))
        factor_of = factor_of * jnp.repeat(jnp.exp(draws), dims[position] // parts).reshape((-1,) + (1,) * (len(dims) - 1 - position))
    return factor_of


def deal_out(rng, own, number, rows, number_of, top, bound, lean):
    order = jax.random.permutation(rng, number_of)
    heavy_load, usual = portions_of(number_of, rows * top, bound, lean, True), portions_of(number_of, rows * top, bound, lean, False)
    places = jnp.arange(number_of)

    def named(lengths, turn):
        used = int((lengths > 0).sum())
        fixed = max(1, used // 4)
        moved = fixed + (places - fixed + turn * (used - fixed)) % max(1, number_of - fixed)
        return jnp.zeros((number_of,), jnp.int32).at[order[jnp.where(places < fixed, places, moved)]].set(jnp.asarray(lengths, jnp.int32))

    lengths = jnp.where(number % 4 == 0, named(heavy_load, number // 4), named(usual, number - number // 4 - 1))
    mixed = jax.random.permutation(jax.random.fold_in(own, 3), number_of)
    donor, receiver = mixed[0:number_of // 2 * 2:2], mixed[1:number_of // 2 * 2:2]
    room = jnp.minimum(lengths[donor] - 1, bound - lengths[receiver]) // 2
    room = jnp.where((donor == order[0]) | (receiver == order[0]) | (lengths[receiver] == 0), 0, jnp.maximum(room, 0))
    moved = jax.random.randint(jax.random.fold_in(own, 4), (number_of // 2,), 0, 1 << 20) % (room + 1)
    lengths = lengths.at[donor].add(-moved).at[receiver].add(moved)
    items = jnp.searchsorted(jnp.cumsum(lengths), jnp.arange(rows * top), side="right").astype(jnp.int32)
    listing = items.reshape(top, rows).T
    listing = listing[jax.random.permutation(jax.random.fold_in(own, 1), rows)]
    turn = jax.random.randint(jax.random.fold_in(own, 2), (rows, 1), 0, top)
    return jnp.take_along_axis(listing, (jnp.arange(top)[None, :] + turn) % top, axis=1)


def portions_of(amount, total, most, lean, full):
    portions = [(1 << 20) // math.isqrt(standing ** lean) + 1 for standing in range(1, amount + 1)]
    largest = most if full else min(most, max(-(-total // amount), total * portions[0] // sum(portions)))
    least = 1 if total - largest >= amount - 1 else 0
    given, rest = [largest] + [least] * (amount - 1), total - largest - least * (amount - 1)
    while rest > 0:
        candidates = [i for i in range(1, amount) if given[i] < largest] or [i for i in range(1, amount) if given[i] < most]
        whole, left = sum([portions[i] for i in candidates]), rest
        for i in candidates:
            addition = min(most - given[i], max(1, left * portions[i] // whole), rest)
            given[i] = given[i] + addition
            rest = rest - addition
    return np.array(given)


def gaussian(own_key, shape, spread, bound, cuts=(), kind=jnp.bfloat16):
    result = jax.random.normal(own_key, shape, jnp.float32) * spread
    if len(cuts) > 0:
        result = block_levels(own_key, shape, cuts, -0.22, 0.18) * result
    return jnp.clip(result, min=-bound, max=bound).astype(kind)


def setup_inputs(seed: int = 0) -> dict:
    streams_of = jax.random.split(jax.random.key(seed), 7)
    q_panel = gaussian(streams_of[0], (N_ROWS, NCB * TILE, RANK), 1.0, 6.0, ((0, 8), (1, 64)))
    tiles = gaussian(streams_of[1], (N_BLK, N_ROWS, TILES_DEV, TILE, TILE), (TPB * NCB * TILE // RB_DEV) ** -0.5, 0.078125, ((0, 64), (1, 8)))
    tile_rows = with_ends(jax.random.randint(streams_of[2], (N_BLK, N_ROWS, TILES_DEV), 0, RBG), jax.random.fold_in(streams_of[2], 1), 0, RBG - 1).astype(jnp.int32)
    tile_cols_keys = jax.random.split(jax.random.fold_in(streams_of[3], 1), N_BLK * N_ROWS * TILES_DEV // TILES_DEV)
    tile_cols_turns = jax.random.permutation(jax.random.fold_in(streams_of[3], 3), N_BLK * N_ROWS * TILES_DEV // TILES_DEV)
    tile_cols = jax.vmap(lambda own, number: deal_out(jax.random.fold_in(streams_of[3], 2), own, number, TILES_DEV, NCB, 1, MOST, 2))(tile_cols_keys, tile_cols_turns).reshape((N_BLK, N_ROWS, TILES_DEV, 1))
    tile_count = draw_tile_count(jax.random.fold_in(streams_of[6], 71), 0)
    owner_map = jax.vmap(lambda own: jax.random.permutation(own, RBG))(jax.random.split(streams_of[5], N_BLK)).reshape((N_BLK, RBG)).astype(jnp.int32)
    return {"q_panel": q_panel, "tiles": tiles, "tile_rows": tile_rows, "tile_cols": tile_cols, "tile_count": tile_count, "owner_map": owner_map}


def reference(q_panel, tiles, tile_rows, tile_cols, tile_count, owner_map):
    q_blocks = q_panel.reshape(N_ROWS, NCB, TILE, RANK)
    active = (jnp.arange(TILES_DEV, dtype=jnp.int32)[None, None, :] < tile_count[:, :, None]).astype(jnp.float32)
    column_ids = tile_cols[..., 0]
    class_index = jnp.arange(N_ROWS, dtype=jnp.int32)[:, None]

    def forward(group):
        chosen = q_blocks[class_index, column_ids[group]]
        product = jnp.einsum("rtij,rtjk->rtik", tiles[group].astype(jnp.float32), chosen.astype(jnp.float32), precision=lax.Precision.HIGHEST)
        product = product * active[group][:, :, None, None]
        return jnp.zeros((RBG, TILE, RANK), jnp.float32).at[tile_rows[group]].add(product)

    y_full = lax.map(forward, jnp.arange(N_BLK, dtype=jnp.int32)).astype(jnp.bfloat16)
    group_index = jnp.arange(N_BLK, dtype=jnp.int32)[:, None]
    y_slots = jnp.zeros((N_BLK, RBG, TILE, RANK), jnp.bfloat16).at[group_index, owner_map].set(y_full)
    y_basis = y_slots.reshape(N_BLK, RBG * TILE, RANK)

    def backward(running, group):
        chosen = y_full[group][tile_rows[group]]
        product = jnp.einsum("rtji,rtjk->rtik", tiles[group].astype(jnp.float32), chosen.astype(jnp.float32), precision=lax.Precision.HIGHEST)
        product = product * active[group][:, :, None, None]
        return running.at[class_index, column_ids[group]].add(product), None

    start_sum = jnp.zeros((N_ROWS, NCB, TILE, RANK), jnp.float32)
    z_blocks, _ = lax.scan(backward, start_sum, jnp.arange(N_BLK, dtype=jnp.int32))
    return y_basis, z_blocks.reshape(N_ROWS, NCB * TILE, RANK)
```

```python
import jax
import jax.numpy as jnp
from jax import lax
from jax.experimental import pallas as pl
from jax.experimental.pallas import tpu as pltpu
from jax.sharding import PartitionSpec as P

MESH = pl.DeviceIdType.MESH
NZ, NY, NC = 8, 4, 2
NH, NX = 2, 4
CH = 4
GROUP = 4
F32 = jnp.float32
BF16 = jnp.bfloat16


def blk_of(z, y, c):
    return (z * NY + y) * NC + c


def blk_position():
    b = lax.axis_index("blk")
    return b // (NY * NC), (b // NC) % NY, b % NC


def greet(peers):
    barrier = pltpu.get_barrier_semaphore()
    for peer in peers:
        pl.semaphore_signal(barrier, inc=1, device_id=peer, device_id_type=MESH)
    pl.semaphore_wait(barrier, len(peers))


def remote(src, dst, send, recv, peer):
    return pltpu.make_async_remote_copy(
        src_ref=src, dst_ref=dst, send_sem=send, recv_sem=recv, device_id=peer, device_id_type=MESH
    )


def blk_peers(z, y, c, r):
    return (
        [(blk_of((z + d) % NZ, y, c), r) for d in range(1, NZ)]
        + [(blk_of(z, (y + e) % NY, c), r) for e in range(1, NY)]
        + [(blk_of(z, y, 1 - c), r)]
    )


def gather_kernel(q_ref, out_ref, lsem, sz, rz, sy, ry, sc, rc):
    z, y, c = blk_position()
    r = lax.axis_index("rows")
    greet(blk_peers(z, y, c, r))
    partner = (blk_of(z, y, 1 - c), r)
    own = pltpu.make_async_copy(q_ref, out_ref.at[z, y, c], lsem)
    own.start()
    sent = []

    def send(src, dst, s, v, peer):
        copy = remote(src, dst, s, v, peer)
        copy.start()
        sent.append(copy)

    for d in (4, 3, 5, 2, 6, 1, 7):
        send(q_ref, out_ref.at[z, y, c], sz.at[d], rz.at[d], (blk_of((z + d) % NZ, y, c), r))
    order = (0, 1, 7, 2, 6, 3, 5, 4)
    for d in order:
        zs = (z + NZ - d) % NZ
        spot = out_ref.at[zs, y, c]
        src = q_ref if d == 0 else spot
        if d:
            remote(spot, spot, sz.at[d], rz.at[d], partner).wait_recv()
        for e in (2, 1, 3):
            send(src, spot, sy.at[d * NY + e], ry.at[d * NY + e], (blk_of(z, (y + e) % NY, c), r))
        send(src, spot, sc.at[d * NY], rc.at[d * NY], partner)
    for d in order:
        zs = (z + NZ - d) % NZ
        for e in (1, 3, 2):
            k = d * NY + e
            spot = out_ref.at[zs, (y + NY - e) % NY, c]
            remote(spot, spot, sy.at[k], ry.at[k], partner).wait_recv()
            send(spot, spot, sc.at[k], rc.at[k], partner)
    for d in order:
        zs = (z + NZ - d) % NZ
        for e in range(NY):
            k = d * NY + e
            spot = out_ref.at[zs, (y + NY - e) % NY, 1 - c]
            remote(spot, spot, sc.at[k], rc.at[k], partner).wait_recv()
    own.wait()
    for copy in sent:
        copy.wait_send()


def exchange_kernel(part_ref, own_ref, all_ref, rx, hs, hr, s1, v1, s2, v2, s3, v3, s4, v4):
    b = lax.axis_index("blk")
    r = lax.axis_index("rows")
    h, x = r // NX, r % NX
    across = (b, (1 - h) * NX + x)
    beside = [None] + [(b, h * NX + (x + d) % NX) for d in range(1, NX)]
    greet(beside[1:] + [across])
    sent = []

    def send(src, dst, s, v, peer):
        copy = remote(src, dst, s, v, peer)
        copy.start()
        sent.append(copy)

    def arrived(spot, s, v):
        remote(spot, spot, s, v, across).wait_recv()

    def one(w, k, d):
        return (w * CH + k) * NX + d

    for w in range(2):
        half = 1 - h if w == 0 else h
        for k in range(CH):
            for d in (2, 1, 3):
                i = one(w, k, d)
                send(part_ref.at[half, (x + d) % NX, k], rx.at[i], s1.at[i], v1.at[i], beside[d])
    for k in range(CH):
        total = part_ref[1 - h, x, k]
        for d in (1, 3, 2):
            i = one(0, k, d)
            arrived(rx.at[i], s1.at[i], v1.at[i])
            total = total + rx[i]
        hs[k] = total
        send(hs.at[k], hr.at[k], s2.at[k], v2.at[k], across)
    for k in range(CH):
        total = part_ref[h, x, k]
        for d in (1, 3, 2):
            i = one(1, k, d)
            arrived(rx.at[i], s1.at[i], v1.at[i])
            total = total + rx[i]
        arrived(hr.at[k], s2.at[k], v2.at[k])
        rounded = (total + hr[k]).astype(BF16)
        own_ref[k] = rounded
        all_ref[h, x, k] = rounded
        spot = all_ref.at[h, x, k]
        send(spot, spot, s3.at[k], v3.at[k], across)
        for d in (2, 1, 3):
            i = one(0, k, d)
            send(spot, spot, s4.at[i], v4.at[i], beside[d])
    for k in range(CH):
        spot = all_ref.at[1 - h, x, k]
        arrived(spot, s3.at[k], v3.at[k])
        for d in (2, 1, 3):
            i = one(1, k, d)
            send(spot, spot, s4.at[i], v4.at[i], beside[d])
    for w in range(2):
        half = h if w == 0 else 1 - h
        for k in range(CH):
            for d in (1, 3, 2):
                i = one(w, k, d)
                arrived(all_ref.at[half, (x + NX - d) % NX, k], s4.at[i], v4.at[i])
    for copy in sent:
        copy.wait_send()


def scatter_kernel(part_ref, out_ref, rcore, acc, ryy, acc2, rzz, sc, vc, sy, vy, sz, vz):
    z, y, c = blk_position()
    r = lax.axis_index("rows")
    greet(blk_peers(z, y, c, r))
    partner = (blk_of(z, y, 1 - c), r)
    sent = []

    def send(src, dst, s, v, peer):
        copy = remote(src, dst, s, v, peer)
        copy.start()
        sent.append(copy)

    def arrived(spot, s, v):
        remote(spot, spot, s, v, partner).wait_recv()

    order = (4, 3, 5, 2, 6, 1, 7, 0)
    for d in order:
        send(part_ref.at[(z + d) % NZ, :, 1 - c], rcore.at[d], sc.at[d], vc.at[d], partner)
    for d in order:
        to = (z + d) % NZ
        arrived(rcore.at[d], sc.at[d], vc.at[d])
        for e in (2, 1, 3, 0):
            k = d * NY + e
            ye = (y + e) % NY
            acc[k] = part_ref[to, ye, c] + rcore[d, ye]
            if e:
                send(acc.at[k], ryy.at[k], sy.at[k], vy.at[k], (blk_of(z, ye, c), r))
    for d in order:
        total = acc[d * NY]
        for e in (1, 3, 2):
            k = d * NY + e
            arrived(ryy.at[k], sy.at[k], vy.at[k])
            total = total + ryy[k]
        acc2[d] = total
        if d:
            send(acc2.at[d], rzz.at[d], sz.at[d], vz.at[d], (blk_of((z + d) % NZ, y, c), r))
    total = acc2[0]
    for d in (1, 7, 2, 6, 3, 5, 4):
        arrived(rzz.at[d], sz.at[d], vz.at[d])
        total = total + rzz[d]
    out_ref[...] = total
    for copy in sent:
        copy.wait_send()


def forward_kernel(count_ref, rows_ref, cols_ref, owner_ref, tiles_ref, q_ref, out_ref):
    out_ref[...] = jnp.zeros_like(out_ref)
    count = count_ref[0]

    def step(g, carry):
        for i in range(GROUP):
            t = g * GROUP + i
            slot, col = owner_ref[rows_ref[t]], cols_ref[t]
            term = jnp.dot(tiles_ref[t], q_ref[col], preferred_element_type=F32)
            out_ref[slot] += jnp.where(t < count, term, 0.0)
        return carry

    lax.fori_loop(0, (count + GROUP - 1) // GROUP, step, 0)


def backward_kernel(count_ref, rows_ref, cols_ref, owner_ref, tiles_ref, y_ref, out_ref):
    out_ref[...] = jnp.zeros_like(out_ref)
    count = count_ref[0]

    def step(g, carry):
        for i in range(GROUP):
            t = g * GROUP + i
            slot, col = owner_ref[rows_ref[t]], cols_ref[t]
            term = lax.dot_general(
                tiles_ref[t], y_ref[slot], (((0,), (0,)), ((), ())), preferred_element_type=F32
            )
            out_ref[col] += jnp.where(t < count, term, 0.0)
        return carry

    lax.fori_loop(0, (count + GROUP - 1) // GROUP, step, 0)


def vmem(n):
    return [pl.BlockSpec(memory_space=pltpu.VMEM)] * n


def talk(kernel, cid, outs, scratch, *args):
    single = not isinstance(outs, tuple)
    return pl.pallas_call(
        kernel,
        out_shape=outs,
        in_specs=vmem(len(args)),
        out_specs=vmem(1)[0] if single else tuple(vmem(len(outs))),
        scratch_shapes=scratch,
        compiler_params=pltpu.CompilerParams(
            collective_id=cid, has_side_effects=True, vmem_limit_bytes=32 << 20
        ),
    )(*args)


def tile_pass(kernel, shape, scalars, *args):
    return pl.pallas_call(
        kernel,
        out_shape=jax.ShapeDtypeStruct(shape, F32),
        in_specs=[pl.BlockSpec(memory_space=pltpu.SMEM)] * len(scalars) + vmem(len(args)),
        out_specs=vmem(1)[0],
        compiler_params=pltpu.CompilerParams(vmem_limit_bytes=32 << 20),
    )(*scalars, *args)


def dma(*shape):
    return pltpu.SemaphoreType.DMA(shape)


def shards(q_panel, tiles, tile_rows, tile_cols, tile_count, owner_map):
    own_q, rank = q_panel.shape[1:]
    tile_stack = tiles[0, 0]
    size = tile_stack.shape[1]
    blocks = owner_map.shape[1]
    scalars = (tile_count[0], tile_rows[0, 0], tile_cols[0, 0, :, 0], owner_map[0])
    copies = NZ * NY
    q_all = talk(
        gather_kernel, 0,
        jax.ShapeDtypeStruct((NZ, NY, NC, own_q, rank), q_panel.dtype),
        [pltpu.SemaphoreType.DMA] + [dma(NZ)] * 2 + [dma(copies)] * 4,
        q_panel[0],
    )
    ncol = NZ * NY * NC * own_q // size
    part = tile_pass(
        forward_kernel, (blocks, size, rank), scalars, tile_stack, q_all.reshape(ncol, size, rank)
    )
    owned = blocks * size // (NH * NX)
    piece = owned // CH
    y_own, y_all = talk(
        exchange_kernel, 1,
        (
            jax.ShapeDtypeStruct((CH, piece, rank), BF16),
            jax.ShapeDtypeStruct((NH, NX, CH, piece, rank), BF16),
        ),
        [
            pltpu.VMEM((2 * CH * NX, piece, rank), F32),
            pltpu.VMEM((CH, piece, rank), F32),
            pltpu.VMEM((CH, piece, rank), F32),
        ]
        + [dma(2 * CH * NX)] * 2 + [dma(CH)] * 4 + [dma(2 * CH * NX)] * 2,
        part.reshape(NH, NX, CH, piece, rank),
    )
    back = tile_pass(
        backward_kernel, (ncol, size, rank), scalars, tile_stack, y_all.reshape(blocks, size, rank)
    )
    z_own = talk(
        scatter_kernel, 2,
        jax.ShapeDtypeStruct((own_q, rank), F32),
        [
            pltpu.VMEM((NZ, NY, own_q, rank), F32),
            pltpu.VMEM((copies, own_q, rank), F32),
            pltpu.VMEM((copies, own_q, rank), F32),
            pltpu.VMEM((NZ, own_q, rank), F32),
            pltpu.VMEM((NZ, own_q, rank), F32),
        ]
        + [dma(NZ)] * 2 + [dma(copies)] * 2 + [dma(NZ)] * 2,
        back.reshape(NZ, NY, NC, own_q, rank),
    )
    return (y_own.reshape(1, owned, rank), z_own[None])


def solution(mesh):
    placed = (
        P("rows", "blk", None),
        P("blk", "rows", None, None, None),
        P("blk", "rows", None),
        P("blk", "rows", None, None),
        P("blk", "rows"),
        P("blk", None),
    )
    return jax.shard_map(
        shards,
        mesh=mesh,
        in_specs=placed,
        out_specs=(P("blk", "rows", None), P("rows", "blk", None)),
        check_vma=False,
    )
```

```python
import jax
import jax.numpy as jnp
from jax import lax
from jax.experimental import pallas as pl
from jax.experimental.pallas import tpu as pltpu
from jax.sharding import PartitionSpec as P

MESH = pl.DeviceIdType.MESH
NZ, NY, NC = 8, 4, 2
NH, NX = 2, 4
CH = 4
GROUP = 4
STEPS = 32766.0
TINY = 1e-30
F32 = jnp.float32
BF16 = jnp.bfloat16


def blk_of(z, y, c):
    return (z * NY + y) * NC + c


def blk_position():
    b = lax.axis_index("blk")
    return b // (NY * NC), (b // NC) % NY, b % NC


def greet(peers):
    barrier = pltpu.get_barrier_semaphore()
    for peer in peers:
        pl.semaphore_signal(barrier, inc=1, device_id=peer, device_id_type=MESH)
    pl.semaphore_wait(barrier, len(peers))


def remote(src, dst, send, recv, peer):
    return pltpu.make_async_remote_copy(
        src_ref=src, dst_ref=dst, send_sem=send, recv_sem=recv, device_id=peer, device_id_type=MESH
    )


def blk_peers(z, y, c, r):
    return (
        [(blk_of((z + d) % NZ, y, c), r) for d in range(1, NZ)]
        + [(blk_of(z, (y + e) % NY, c), r) for e in range(1, NY)]
        + [(blk_of(z, y, 1 - c), r)]
    )


def pack(piece, whole_ref, scale_ref, i):
    top = jnp.maximum(jnp.max(jnp.abs(piece), axis=0, keepdims=True), TINY)
    scale_ref[i] = top * (1.0 / STEPS)
    whole_ref[i] = jnp.round(piece * (STEPS / top)).astype(jnp.int32).astype(jnp.int16)


def unpack(whole_ref, scale_ref, i):
    return whole_ref[i].astype(jnp.int32).astype(F32) * scale_ref[i]


def gather_kernel(q_ref, out_ref, lsem, sz, rz, sy, ry, sc, rc):
    z, y, c = blk_position()
    r = lax.axis_index("rows")
    greet(blk_peers(z, y, c, r))
    partner = (blk_of(z, y, 1 - c), r)
    own = pltpu.make_async_copy(q_ref, out_ref.at[z, y, c], lsem)
    own.start()
    sent = []

    def send(src, dst, s, v, peer):
        copy = remote(src, dst, s, v, peer)
        copy.start()
        sent.append(copy)

    for d in (4, 3, 5, 2, 6, 1, 7):
        send(q_ref, out_ref.at[z, y, c], sz.at[d], rz.at[d], (blk_of((z + d) % NZ, y, c), r))
    order = (0, 1, 7, 2, 6, 3, 5, 4)
    for d in order:
        zs = (z + NZ - d) % NZ
        spot = out_ref.at[zs, y, c]
        src = q_ref if d == 0 else spot
        if d:
            remote(spot, spot, sz.at[d], rz.at[d], partner).wait_recv()
        for e in (2, 1, 3):
            send(src, spot, sy.at[d * NY + e], ry.at[d * NY + e], (blk_of(z, (y + e) % NY, c), r))
        send(src, spot, sc.at[d * NY], rc.at[d * NY], partner)
    for d in order:
        zs = (z + NZ - d) % NZ
        for e in (1, 3, 2):
            k = d * NY + e
            spot = out_ref.at[zs, (y + NY - e) % NY, c]
            remote(spot, spot, sy.at[k], ry.at[k], partner).wait_recv()
            send(spot, spot, sc.at[k], rc.at[k], partner)
    for d in order:
        zs = (z + NZ - d) % NZ
        for e in range(NY):
            k = d * NY + e
            spot = out_ref.at[zs, (y + NY - e) % NY, 1 - c]
            remote(spot, spot, sc.at[k], rc.at[k], partner).wait_recv()
    own.wait()
    for copy in sent:
        copy.wait_send()


def exchange_kernel(
    part_ref, all_ref, tx, tm, rx, rm, hs, hm, hr, hn,
    s1, v1, s1m, v1m, s2, v2, s2m, v2m, s3, v3, s4, v4,
):
    b = lax.axis_index("blk")
    r = lax.axis_index("rows")
    h, x = r // NX, r % NX
    across = (b, (1 - h) * NX + x)
    beside = [None] + [(b, h * NX + (x + d) % NX) for d in range(1, NX)]
    greet(beside[1:] + [across])
    sent = []

    def send(src, dst, s, v, peer):
        copy = remote(src, dst, s, v, peer)
        copy.start()
        sent.append(copy)

    def arrived(spot, s, v):
        remote(spot, spot, s, v, across).wait_recv()

    def one(w, k, d):
        return (w * CH + k) * NX + d

    for w in range(2):
        half = 1 - h if w == 0 else h
        for k in range(CH):
            for d in (2, 1, 3):
                i = one(w, k, d)
                pack(part_ref[half, (x + d) % NX, k], tx, tm, i)
                send(tm.at[i], rm.at[i], s1m.at[i], v1m.at[i], beside[d])
                send(tx.at[i], rx.at[i], s1.at[i], v1.at[i], beside[d])

    def summed(w, half, k):
        total = part_ref[half, x, k]
        for d in (1, 3, 2):
            i = one(w, k, d)
            arrived(rm.at[i], s1m.at[i], v1m.at[i])
            arrived(rx.at[i], s1.at[i], v1.at[i])
            total = total + unpack(rx, rm, i)
        return total

    for k in range(CH):
        pack(summed(0, 1 - h, k), hs, hm, k)
        send(hm.at[k], hn.at[k], s2m.at[k], v2m.at[k], across)
        send(hs.at[k], hr.at[k], s2.at[k], v2.at[k], across)
    for k in range(CH):
        total = summed(1, h, k)
        arrived(hn.at[k], s2m.at[k], v2m.at[k])
        arrived(hr.at[k], s2.at[k], v2.at[k])
        all_ref[h, x, k] = (total + unpack(hr, hn, k)).astype(BF16)
        spot = all_ref.at[h, x, k]
        send(spot, spot, s3.at[k], v3.at[k], across)
        for d in (2, 1, 3):
            i = one(0, k, d)
            send(spot, spot, s4.at[i], v4.at[i], beside[d])
    for k in range(CH):
        spot = all_ref.at[1 - h, x, k]
        arrived(spot, s3.at[k], v3.at[k])
        for d in (2, 1, 3):
            i = one(1, k, d)
            send(spot, spot, s4.at[i], v4.at[i], beside[d])
    for w in range(2):
        half = h if w == 0 else 1 - h
        for k in range(CH):
            for d in (1, 3, 2):
                i = one(w, k, d)
                arrived(all_ref.at[half, (x + NX - d) % NX, k], s4.at[i], v4.at[i])
    for copy in sent:
        copy.wait_send()


def scatter_kernel(
    part_ref, out_ref, rcore, acc, ty, tym, ryy, rym, tz, tzm, rzz, rzm,
    sc, vc, sy, vy, sym, vym, sz, vz, szm, vzm,
):
    z, y, c = blk_position()
    r = lax.axis_index("rows")
    greet(blk_peers(z, y, c, r))
    partner = (blk_of(z, y, 1 - c), r)
    sent = []

    def send(src, dst, s, v, peer):
        copy = remote(src, dst, s, v, peer)
        copy.start()
        sent.append(copy)

    def arrived(spot, s, v):
        remote(spot, spot, s, v, partner).wait_recv()

    order = (4, 3, 5, 2, 6, 1, 7, 0)
    for d in order:
        send(part_ref.at[(z + d) % NZ, :, 1 - c], rcore.at[d], sc.at[d], vc.at[d], partner)
    for d in order:
        to = (z + d) % NZ
        arrived(rcore.at[d], sc.at[d], vc.at[d])
        for e in (2, 1, 3, 0):
            k = d * NY + e
            ye = (y + e) % NY
            total = part_ref[to, ye, c] + rcore[d, ye]
            if e:
                peer = (blk_of(z, ye, c), r)
                pack(total, ty, tym, k)
                send(tym.at[k], rym.at[k], sym.at[k], vym.at[k], peer)
                send(ty.at[k], ryy.at[k], sy.at[k], vy.at[k], peer)
            else:
                acc[d] = total
    for d in order:
        total = acc[d]
        for e in (1, 3, 2):
            k = d * NY + e
            arrived(rym.at[k], sym.at[k], vym.at[k])
            arrived(ryy.at[k], sy.at[k], vy.at[k])
            total = total + unpack(ryy, rym, k)
        if d:
            peer = (blk_of((z + d) % NZ, y, c), r)
            pack(total, tz, tzm, d)
            send(tzm.at[d], rzm.at[d], szm.at[d], vzm.at[d], peer)
            send(tz.at[d], rzz.at[d], sz.at[d], vz.at[d], peer)
    for d in (1, 7, 2, 6, 3, 5, 4):
        arrived(rzm.at[d], szm.at[d], vzm.at[d])
        arrived(rzz.at[d], sz.at[d], vz.at[d])
        total = total + unpack(rzz, rzm, d)
    out_ref[...] = total
    for copy in sent:
        copy.wait_send()


def forward_kernel(count_ref, rows_ref, cols_ref, owner_ref, tiles_ref, q_ref, out_ref):
    out_ref[...] = jnp.zeros_like(out_ref)
    count = count_ref[0]

    def step(g, carry):
        for i in range(GROUP):
            t = g * GROUP + i
            slot, col = owner_ref[rows_ref[t]], cols_ref[t]
            term = jnp.dot(tiles_ref[t], q_ref[col], preferred_element_type=F32)
            out_ref[slot] += jnp.where(t < count, term, 0.0)
        return carry

    lax.fori_loop(0, (count + GROUP - 1) // GROUP, step, 0)


def backward_kernel(count_ref, rows_ref, cols_ref, owner_ref, tiles_ref, y_ref, out_ref, own_ref):
    first = lax.axis_index("rows") * own_ref.shape[0]
    for k in range(own_ref.shape[0]):
        own_ref[k] = y_ref[first + k]
    out_ref[...] = jnp.zeros_like(out_ref)
    count = count_ref[0]

    def step(g, carry):
        for i in range(GROUP):
            t = g * GROUP + i
            slot, col = owner_ref[rows_ref[t]], cols_ref[t]
            term = lax.dot_general(
                tiles_ref[t], y_ref[slot], (((0,), (0,)), ((), ())), preferred_element_type=F32
            )
            out_ref[col] += jnp.where(t < count, term, 0.0)
        return carry

    lax.fori_loop(0, (count + GROUP - 1) // GROUP, step, 0)


def vmem(n):
    return [pl.BlockSpec(memory_space=pltpu.VMEM)] * n


def talk(kernel, cid, outs, scratch, *args):
    single = not isinstance(outs, tuple)
    cost = pl.CostEstimate(flops=0, bytes_accessed=64 << 20, transcendentals=0)
    return pl.pallas_call(
        kernel,
        out_shape=outs,
        in_specs=vmem(len(args)),
        out_specs=vmem(1)[0] if single else tuple(vmem(len(outs))),
        scratch_shapes=scratch,
        cost_estimate=cost,
        compiler_params=pltpu.CompilerParams(
            collective_id=cid, has_side_effects=True, vmem_limit_bytes=32 << 20
        ),
    )(*args)


def tile_pass(kernel, shape, scalars, *args):
    return pl.pallas_call(
        kernel,
        out_shape=shape,
        in_specs=[pl.BlockSpec(memory_space=pltpu.SMEM)] * len(scalars) + vmem(len(args)),
        out_specs=tuple(vmem(len(shape))),
        compiler_params=pltpu.CompilerParams(vmem_limit_bytes=32 << 20),
    )(*scalars, *args)


def dma(*shape):
    return pltpu.SemaphoreType.DMA(shape)


def shards(q_panel, tiles, tile_rows, tile_cols, tile_count, owner_map):
    own_q, rank = q_panel.shape[1:]
    tile_stack = tiles[0, 0]
    size = tile_stack.shape[1]
    blocks = owner_map.shape[1]
    scalars = (tile_count[0], tile_rows[0, 0], tile_cols[0, 0, :, 0], owner_map[0])
    copies = NZ * NY
    q_all = talk(
        gather_kernel, 0,
        jax.ShapeDtypeStruct((NZ, NY, NC, own_q, rank), q_panel.dtype),
        [pltpu.SemaphoreType.DMA] + [dma(NZ)] * 2 + [dma(copies)] * 4,
        q_panel[0],
    )
    ncol = NZ * NY * NC * own_q // size
    (part,) = tile_pass(
        forward_kernel,
        (jax.ShapeDtypeStruct((blocks, size, rank), F32),),
        scalars, tile_stack, q_all.reshape(ncol, size, rank),
    )
    owned = blocks * size // (NH * NX)
    piece = owned // CH

    def sixteen(n, rows):
        return [pltpu.VMEM((n, rows, rank), jnp.int16), pltpu.VMEM((n, 1, rank), F32)]

    pieces = 2 * CH * NX
    y_all = talk(
        exchange_kernel, 1,
        jax.ShapeDtypeStruct((NH, NX, CH, piece, rank), BF16),
        sixteen(pieces, piece) * 2 + sixteen(CH, piece) * 2
        + [dma(pieces)] * 4 + [dma(CH)] * 4 + [dma(CH)] * 2 + [dma(pieces)] * 2,
        part.reshape(NH, NX, CH, piece, rank),
    )
    back, y_own = tile_pass(
        backward_kernel,
        (
            jax.ShapeDtypeStruct((ncol, size, rank), F32),
            jax.ShapeDtypeStruct((owned // size, size, rank), BF16),
        ),
        scalars, tile_stack, y_all.reshape(blocks, size, rank),
    )
    z_own = talk(
        scatter_kernel, 2,
        jax.ShapeDtypeStruct((own_q, rank), F32),
        [
            pltpu.VMEM((NZ, NY, own_q, rank), F32),
            pltpu.VMEM((NZ, own_q, rank), F32),
        ]
        + sixteen(copies, own_q) * 2 + sixteen(NZ, own_q) * 2
        + [dma(NZ)] * 2 + [dma(copies)] * 4 + [dma(NZ)] * 4,
        back.reshape(NZ, NY, NC, own_q, rank),
    )
    return (y_own.reshape(1, owned, rank), z_own[None])


def solution(mesh):
    placed = (
        P("rows", "blk", None),
        P("blk", "rows", None, None, None),
        P("blk", "rows", None),
        P("blk", "rows", None, None),
        P("blk", "rows"),
        P("blk", None),
    )
    return jax.shard_map(
        shards,
        mesh=mesh,
        in_specs=placed,
        out_specs=(P("blk", "rows", None), P("rows", "blk", None)),
        check_vma=False,
    )
```

```python
import jax
import jax.numpy as jnp
from jax import lax
from jax.experimental import pallas as pl
from jax.experimental.pallas import tpu as pltpu
from jax.sharding import PartitionSpec as P

MESH = pl.DeviceIdType.MESH
NZ, NY, NC = 8, 4, 2
NH, NX = 2, 4
CH = 4
GROUP = 4
STEPS = 32766.0
TINY = 1e-30
GRANT = 49 << 20
F32 = jnp.float32
BF16 = jnp.bfloat16


def blk_of(z, y, c):
    return (z * NY + y) * NC + c


def blk_position():
    b = lax.axis_index("blk")
    return b // (NY * NC), (b // NC) % NY, b % NC


def call(peers):
    for peer in peers:
        pl.semaphore_signal(
            pltpu.get_barrier_semaphore(), inc=1, device_id=peer, device_id_type=MESH
        )


def listen(peers):
    pl.semaphore_wait(pltpu.get_barrier_semaphore(), len(peers))


def remote(src, dst, send, recv, peer):
    return pltpu.make_async_remote_copy(
        src_ref=src, dst_ref=dst, send_sem=send, recv_sem=recv, device_id=peer, device_id_type=MESH
    )


def blk_peers(z, y, c, r):
    return (
        [(blk_of((z + d) % NZ, y, c), r) for d in range(1, NZ)]
        + [(blk_of(z, (y + e) % NY, c), r) for e in range(1, NY)]
        + [(blk_of(z, y, 1 - c), r)]
    )


def pack(piece, whole_ref, scale_ref, i):
    top = jnp.maximum(jnp.max(jnp.abs(piece), axis=0, keepdims=True), TINY)
    scale_ref[i] = top * (1.0 / STEPS)
    whole_ref[i] = jnp.round(piece * (STEPS / top)).astype(jnp.int32).astype(jnp.int16)


def unpack(whole_ref, scale_ref, i):
    return whole_ref[i].astype(jnp.int32).astype(F32) * scale_ref[i]


def gather_kernel(q_ref, held_ref, out_ref, moved_ref, lsem, sz, rz, sy, ry, sc, rc):
    z, y, c = blk_position()
    r = lax.axis_index("rows")
    call(blk_peers(z, y, c, r))
    local = pltpu.make_async_copy(held_ref, moved_ref, lsem.at[1])
    local.start()
    listen(blk_peers(z, y, c, r))
    partner = (blk_of(z, y, 1 - c), r)
    own = pltpu.make_async_copy(q_ref, out_ref.at[z, y, c], lsem.at[0])
    own.start()
    sent = []

    def send(src, dst, s, v, peer):
        copy = remote(src, dst, s, v, peer)
        copy.start()
        sent.append(copy)

    for d in (4, 3, 5, 2, 6, 1, 7):
        send(q_ref, out_ref.at[z, y, c], sz.at[d], rz.at[d], (blk_of((z + d) % NZ, y, c), r))
    order = (0, 1, 7, 2, 6, 3, 5, 4)
    for d in order:
        zs = (z + NZ - d) % NZ
        spot = out_ref.at[zs, y, c]
        src = q_ref if d == 0 else spot
        if d:
            remote(spot, spot, sz.at[d], rz.at[d], partner).wait_recv()
        for e in (2, 1, 3):
            send(src, spot, sy.at[d * NY + e], ry.at[d * NY + e], (blk_of(z, (y + e) % NY, c), r))
        send(src, spot, sc.at[d * NY], rc.at[d * NY], partner)
    for d in order:
        zs = (z + NZ - d) % NZ
        for e in (1, 3, 2):
            k = d * NY + e
            spot = out_ref.at[zs, (y + NY - e) % NY, c]
            remote(spot, spot, sy.at[k], ry.at[k], partner).wait_recv()
            send(spot, spot, sc.at[k], rc.at[k], partner)
    for d in order:
        zs = (z + NZ - d) % NZ
        for e in range(NY):
            k = d * NY + e
            spot = out_ref.at[zs, (y + NY - e) % NY, 1 - c]
            remote(spot, spot, sc.at[k], rc.at[k], partner).wait_recv()
    own.wait()
    local.wait()
    for copy in sent:
        copy.wait_send()


def exchange_kernel(
    part_ref, all_ref, tx, tm, rx, rm, hs, hm, hr, hn,
    s1, v1, s1m, v1m, s2, v2, s2m, v2m, s3, v3,
):
    b = lax.axis_index("blk")
    r = lax.axis_index("rows")
    h, x = r // NX, r % NX
    across = (b, (1 - h) * NX + x)
    beside = [None] + [(b, h * NX + (x + d) % NX) for d in range(1, NX)]
    peers = beside[1:] + [across]
    call(peers)
    order = [(k, w) for k in range(CH) for w in range(NH)]
    sent = []

    def send(src, dst, s, v, peer):
        copy = remote(src, dst, s, v, peer)
        copy.start()
        sent.append(copy)

    def arrived(spot, s, v):
        remote(spot, spot, s, v, across).wait_recv()

    for k, w in order:
        for d in (2, 1, 3):
            pack(part_ref[w, (x + d) % NX, k], tx, tm, (k * NH + w) * NX + d)
    listen(peers)
    for k, w in order:
        for d in (2, 1, 3):
            i = (k * NH + w) * NX + d
            send(tm.at[i], rm.at[i], s1m.at[i], v1m.at[i], beside[d])
            send(tx.at[i], rx.at[i], s1.at[i], v1.at[i], beside[d])
    for k, w in order:
        j = k * NH + w
        total = part_ref[w, x, k]
        for d in (1, 3, 2):
            i = j * NX + d
            arrived(rm.at[i], s1m.at[i], v1m.at[i])
            arrived(rx.at[i], s1.at[i], v1.at[i])
            total = total + unpack(rx, rm, i)
        pack(total, hs, hm, j)
        send(hm.at[j], hn.at[j], s2m.at[j], v2m.at[j], across)
        send(hs.at[j], hr.at[j], s2.at[j], v2.at[j], across)
    for k, w in order:
        j = k * NH + w
        arrived(hn.at[j], s2m.at[j], v2m.at[j])
        arrived(hr.at[j], s2.at[j], v2.at[j])
        all_ref[w, x, k] = (unpack(hs, hm, j) + unpack(hr, hn, j)).astype(BF16)
        spot = all_ref.at[w, x, k]
        for d in (2, 1, 3):
            i = j * NX + d
            send(spot, spot, s3.at[i], v3.at[i], beside[d])
    for k, w in order:
        for d in (1, 3, 2):
            i = (k * NH + w) * NX + d
            arrived(all_ref.at[w, (x + NX - d) % NX, k], s3.at[i], v3.at[i])
    for copy in sent:
        copy.wait_send()


def scatter_kernel(
    part_ref, out_ref, rcore, acc, ty, tym, ryy, rym, tz, tzm, rzz, rzm,
    sc, vc, sy, vy, sym, vym, sz, vz, szm, vzm,
):
    z, y, c = blk_position()
    r = lax.axis_index("rows")
    call(blk_peers(z, y, c, r))
    listen(blk_peers(z, y, c, r))
    partner = (blk_of(z, y, 1 - c), r)
    sent = []

    def send(src, dst, s, v, peer):
        copy = remote(src, dst, s, v, peer)
        copy.start()
        sent.append(copy)

    def arrived(spot, s, v):
        remote(spot, spot, s, v, partner).wait_recv()

    order = (4, 3, 5, 2, 6, 1, 7, 0)
    for d in order:
        send(part_ref.at[(z + d) % NZ, :, 1 - c], rcore.at[d], sc.at[d], vc.at[d], partner)
    for d in order:
        to = (z + d) % NZ
        arrived(rcore.at[d], sc.at[d], vc.at[d])
        for e in (2, 1, 3, 0):
            k = d * NY + e
            ye = (y + e) % NY
            total = part_ref[to, ye, c] + rcore[d, ye]
            if e:
                peer = (blk_of(z, ye, c), r)
                pack(total, ty, tym, k)
                send(tym.at[k], rym.at[k], sym.at[k], vym.at[k], peer)
                send(ty.at[k], ryy.at[k], sy.at[k], vy.at[k], peer)
            else:
                acc[d] = total
    for d in order:
        total = acc[d]
        for e in (1, 3, 2):
            k = d * NY + e
            arrived(rym.at[k], sym.at[k], vym.at[k])
            arrived(ryy.at[k], sy.at[k], vy.at[k])
            total = total + unpack(ryy, rym, k)
        if d:
            peer = (blk_of((z + d) % NZ, y, c), r)
            pack(total, tz, tzm, d)
            send(tzm.at[d], rzm.at[d], szm.at[d], vzm.at[d], peer)
            send(tz.at[d], rzz.at[d], sz.at[d], vz.at[d], peer)
    for d in (1, 7, 2, 6, 3, 5, 4):
        arrived(rzm.at[d], szm.at[d], vzm.at[d])
        arrived(rzz.at[d], sz.at[d], vz.at[d])
        total = total + unpack(rzz, rzm, d)
    out_ref[...] = total
    for copy in sent:
        copy.wait_send()


def forward_kernel(meta_ref, tiles_ref, q_ref, out_ref):
    out_ref[...] = jnp.zeros_like(out_ref)
    held = tiles_ref.shape[0]
    count = meta_ref[meta_ref.shape[0] - 1]

    def step(g, carry):
        for i in range(GROUP):
            t = g * GROUP + i
            slot, col = meta_ref[2 * held + meta_ref[t]], meta_ref[held + t]
            term = jnp.dot(tiles_ref[t], q_ref[col], preferred_element_type=F32)
            out_ref[slot] += jnp.where(t < count, term, 0.0)
        return carry

    lax.fori_loop(0, (count + GROUP - 1) // GROUP, step, 0)


def backward_kernel(meta_ref, tiles_ref, y_ref, out_ref, own_ref):
    first = lax.axis_index("rows") * own_ref.shape[0]
    for k in range(own_ref.shape[0]):
        own_ref[k] = y_ref[first + k]
    out_ref[...] = jnp.zeros_like(out_ref)
    held = tiles_ref.shape[0]
    count = meta_ref[meta_ref.shape[0] - 1]

    def step(g, carry):
        for i in range(GROUP):
            t = g * GROUP + i
            slot, col = meta_ref[2 * held + meta_ref[t]], meta_ref[held + t]
            term = lax.dot_general(
                tiles_ref[t], y_ref[slot], (((0,), (0,)), ((), ())), preferred_element_type=F32
            )
            out_ref[col] += jnp.where(t < count, term, 0.0)
        return carry

    lax.fori_loop(0, (count + GROUP - 1) // GROUP, step, 0)


def vmem(n):
    return [pl.BlockSpec(memory_space=pltpu.VMEM)] * n


def talk(kernel, cid, outs, scratch, *args):
    single = not isinstance(outs, tuple)
    cost = pl.CostEstimate(flops=0, bytes_accessed=64 << 20, transcendentals=0)
    return pl.pallas_call(
        kernel,
        out_shape=outs,
        in_specs=vmem(len(args)),
        out_specs=vmem(1)[0] if single else tuple(vmem(len(outs))),
        scratch_shapes=scratch,
        cost_estimate=cost,
        compiler_params=pltpu.CompilerParams(
            collective_id=cid, has_side_effects=True, vmem_limit_bytes=32 << 20
        ),
    )(*args)


def tile_pass(kernel, shape, meta, *args):
    return pl.pallas_call(
        kernel,
        out_shape=shape,
        in_specs=[pl.BlockSpec(memory_space=pltpu.SMEM)] + vmem(len(args)),
        out_specs=tuple(vmem(len(shape))),
        compiler_params=pltpu.CompilerParams(vmem_limit_bytes=32 << 20),
    )(meta, *args)


def dma(*shape):
    return pltpu.SemaphoreType.DMA(shape)


def shards(q_panel, tiles, tile_rows, tile_cols, tile_count, owner_map):
    own_q, rank = q_panel.shape[1:]
    tile_stack = tiles[0, 0]
    size = tile_stack.shape[1]
    blocks = owner_map.shape[1]
    copies = NZ * NY
    meta = jnp.concatenate(
        [tile_rows[0, 0], tile_cols[0, 0, :, 0], owner_map[0], tile_count[0]]
    )
    q_all, tile_stack = pl.pallas_call(
        gather_kernel,
        out_shape=(
            jax.ShapeDtypeStruct((NZ, NY, NC, own_q, rank), q_panel.dtype),
            jax.ShapeDtypeStruct(tile_stack.shape, tile_stack.dtype),
        ),
        in_specs=vmem(1) + [pl.BlockSpec(memory_space=pltpu.HBM)],
        out_specs=tuple(vmem(2)),
        scratch_shapes=[dma(2)] + [dma(NZ)] * 2 + [dma(copies)] * 4,
        compiler_params=pltpu.CompilerParams(
            collective_id=0, has_side_effects=True, vmem_limit_bytes=GRANT
        ),
    )(q_panel[0], tile_stack)
    ncol = NZ * NY * NC * own_q // size
    (part,) = tile_pass(
        forward_kernel,
        (jax.ShapeDtypeStruct((blocks, size, rank), F32),),
        meta, tile_stack, q_all.reshape(ncol, size, rank),
    )
    owned = blocks * size // (NH * NX)
    piece = owned // CH

    def sixteen(n, rows):
        return [pltpu.VMEM((n, rows, rank), jnp.int16), pltpu.VMEM((n, 1, rank), F32)]

    each = NH * CH
    pieces = each * NX
    y_all = talk(
        exchange_kernel, 1,
        jax.ShapeDtypeStruct((NH, NX, CH, piece, rank), BF16),
        sixteen(pieces, piece) * 2 + sixteen(each, piece) * 2
        + [dma(pieces)] * 4 + [dma(each)] * 4 + [dma(pieces)] * 2,
        part.reshape(NH, NX, CH, piece, rank),
    )
    back, y_own = tile_pass(
        backward_kernel,
        (
            jax.ShapeDtypeStruct((ncol, size, rank), F32),
            jax.ShapeDtypeStruct((owned // size, size, rank), BF16),
        ),
        meta, tile_stack, y_all.reshape(blocks, size, rank),
    )
    z_own = talk(
        scatter_kernel, 2,
        jax.ShapeDtypeStruct((own_q, rank), F32),
        [
            pltpu.VMEM((NZ, NY, own_q, rank), F32),
            pltpu.VMEM((NZ, own_q, rank), F32),
        ]
        + sixteen(copies, own_q) * 2 + sixteen(NZ, own_q) * 2
        + [dma(NZ)] * 2 + [dma(copies)] * 4 + [dma(NZ)] * 4,
        back.reshape(NZ, NY, NC, own_q, rank),
    )
    return (y_own.reshape(1, owned, rank), z_own[None])


def solution(mesh):
    placed = (
        P("rows", "blk", None),
        P("blk", "rows", None, None, None),
        P("blk", "rows", None),
        P("blk", "rows", None, None),
        P("blk", "rows"),
        P("blk", None),
    )
    return jax.shard_map(
        shards,
        mesh=mesh,
        in_specs=placed,
        out_specs=(P("blk", "rows", None), P("rows", "blk", None)),
        check_vma=False,
    )
```

```python
import jax
import jax.numpy as jnp
from jax import lax
from jax.experimental import pallas as pl
from jax.experimental.pallas import tpu as pltpu
from jax.sharding import PartitionSpec as P

MESH = pl.DeviceIdType.MESH
NZ, NY, NC = 8, 4, 2
NH, NX = 2, 4
CH = 4
GROUP = 4
STEPS = 32766.0
TINY = 1e-30
LANES = 128
GRANT = 49 << 20
F32 = jnp.float32
BF16 = jnp.bfloat16


def blk_of(z, y, c):
    return (z * NY + y) * NC + c


def blk_position():
    b = lax.axis_index("blk")
    return b // (NY * NC), (b // NC) % NY, b % NC


def call(peers):
    for peer in peers:
        pl.semaphore_signal(
            pltpu.get_barrier_semaphore(), inc=1, device_id=peer, device_id_type=MESH
        )


def listen(peers):
    pl.semaphore_wait(pltpu.get_barrier_semaphore(), len(peers))


def remote(src, dst, send, recv, peer):
    return pltpu.make_async_remote_copy(
        src_ref=src, dst_ref=dst, send_sem=send, recv_sem=recv, device_id=peer, device_id_type=MESH
    )


def blk_peers(z, y, c, r):
    return (
        [(blk_of((z + d) % NZ, y, c), r) for d in range(1, NZ)]
        + [(blk_of(z, (y + e) % NY, c), r) for e in range(1, NY)]
        + [(blk_of(z, y, 1 - c), r)]
    )


def pack(piece, whole_ref, scale_ref, i):
    top = jnp.maximum(jnp.max(jnp.abs(piece), axis=0, keepdims=True), TINY)
    scale_ref[i] = top * (1.0 / STEPS)
    whole_ref[i] = jnp.round(piece * (STEPS / top)).astype(jnp.int32).astype(jnp.int16)


def unpack(whole_ref, scale_ref, i):
    return whole_ref[i].astype(jnp.int32).astype(F32) * scale_ref[i]


def down(row):
    return jnp.broadcast_to(row, (LANES, LANES)).T


def make_plan(listed_ref, plan_ref):
    lane = lax.broadcasted_iota(jnp.int32, (LANES, LANES), 1).astype(F32)
    deep = lax.broadcasted_iota(jnp.int32, (LANES, LANES), 0).astype(F32)
    rows, cols, owner, count = [listed_ref[i : i + 1, :] for i in range(4)]

    def total(mask, value):
        return jnp.sum(jnp.where(mask, value, 0.0), axis=0, keepdims=True)

    slots = total(deep == rows, down(owner))
    live = lane[0:1] < count
    for at, (mine, other) in enumerate(((slots, cols), (cols, slots))):
        block = jnp.where(live, mine, 1.0 * LANES)
        key = block * LANES + lane[0:1]
        place = total(down(key) < key, 1.0)
        here = down(place) == lane
        before = down(place) == lane - 1.0
        block_down = down(block)
        sorted_block = total(here, block_down)
        keep = jnp.where(total(before, block_down) == sorted_block, 1.0, 0.0)
        keep = jnp.where(lane[0:1] == 0.0, 0.0, keep)
        last = jnp.maximum(total(block_down <= lane, 1.0) - 1.0, 0.0)
        has = jnp.where(total(block_down == lane, 1.0) > 0.0, 1.0, 0.0)
        for i, row in enumerate((total(here, deep), keep, total(here, down(other)), last, has)):
            plan_ref[5 * at + i : 5 * at + i + 1, :] = row.astype(jnp.int32)


def running_sums(plan_ref, first, tiles_ref, from_ref, sums, turned):
    across = (((0,), (0,)), ((), ())) if turned else (((1,), (0,)), ((), ()))

    def step(p, total):
        term = lax.dot_general(
            tiles_ref[plan_ref[first, p]], from_ref[plan_ref[first + 2, p]], across,
            preferred_element_type=F32,
        )
        total = total * plan_ref[first + 1, p].astype(F32) + term
        sums[p] = total
        return total

    start = jnp.zeros(sums.shape[1:], F32)
    lax.fori_loop(0, tiles_ref.shape[0], step, start, unroll=4)


def block_sum(plan_ref, first, sums, i):
    return sums[plan_ref[first + 3, i]] * plan_ref[first + 4, i].astype(F32)


def gather_kernel(q_ref, held_ref, listed_ref, out_ref, moved_ref, plan_ref, lsem, sz, rz, sy, ry, sc, rc):
    z, y, c = blk_position()
    r = lax.axis_index("rows")
    call(blk_peers(z, y, c, r))
    local = pltpu.make_async_copy(held_ref, moved_ref, lsem.at[1])
    local.start()
    make_plan(listed_ref, plan_ref)
    listen(blk_peers(z, y, c, r))
    partner = (blk_of(z, y, 1 - c), r)
    own = pltpu.make_async_copy(q_ref, out_ref.at[z, y, c], lsem.at[0])
    own.start()
    sent = []

    def send(src, dst, s, v, peer):
        copy = remote(src, dst, s, v, peer)
        copy.start()
        sent.append(copy)

    for d in (4, 3, 5, 2, 6, 1, 7):
        send(q_ref, out_ref.at[z, y, c], sz.at[d], rz.at[d], (blk_of((z + d) % NZ, y, c), r))
    order = (0, 1, 7, 2, 6, 3, 5, 4)
    for d in order:
        zs = (z + NZ - d) % NZ
        spot = out_ref.at[zs, y, c]
        src = q_ref if d == 0 else spot
        if d:
            remote(spot, spot, sz.at[d], rz.at[d], partner).wait_recv()
        for e in (2, 1, 3):
            send(src, spot, sy.at[d * NY + e], ry.at[d * NY + e], (blk_of(z, (y + e) % NY, c), r))
        send(src, spot, sc.at[d * NY], rc.at[d * NY], partner)
    for d in order:
        zs = (z + NZ - d) % NZ
        for e in (1, 3, 2):
            k = d * NY + e
            spot = out_ref.at[zs, (y + NY - e) % NY, c]
            remote(spot, spot, sy.at[k], ry.at[k], partner).wait_recv()
            send(spot, spot, sc.at[k], rc.at[k], partner)
    for d in order:
        zs = (z + NZ - d) % NZ
        for e in range(NY):
            k = d * NY + e
            spot = out_ref.at[zs, (y + NY - e) % NY, 1 - c]
            remote(spot, spot, sc.at[k], rc.at[k], partner).wait_recv()
    own.wait()
    local.wait()
    for copy in sent:
        copy.wait_send()


def exchange_kernel(
    plan_ref, tiles_ref, q_ref, all_ref, sums, part_ref, tx, tm, rx, rm, hs, hm, hr, hn,
    s1, v1, s1m, v1m, s2, v2, s2m, v2m, s3, v3,
):
    b = lax.axis_index("blk")
    r = lax.axis_index("rows")
    h, x = r // NX, r % NX
    across = (b, (1 - h) * NX + x)
    beside = [None] + [(b, h * NX + (x + d) % NX) for d in range(1, NX)]
    peers = beside[1:] + [across]
    call(peers)
    piece = part_ref.shape[3]
    order = [(k, w) for k in range(CH) for w in range(NH)]
    sent = []

    def send(src, dst, s, v, peer):
        copy = remote(src, dst, s, v, peer)
        copy.start()
        sent.append(copy)

    def arrived(spot, s, v):
        remote(spot, spot, s, v, across).wait_recv()

    running_sums(plan_ref, 0, tiles_ref, q_ref, sums, False)
    half = CH // 2
    for i in range(NH * NX * 2):
        block = block_sum(plan_ref, 0, sums, i)
        spot = (i // (2 * NX), i // 2 % NX)
        for k in range(half):
            part_ref[(*spot, i % 2 * half + k)] = block[k * piece : (k + 1) * piece]
    for k, w in order:
        for d in (2, 1, 3):
            pack(part_ref[w, (x + d) % NX, k], tx, tm, (k * NH + w) * NX + d)
    listen(peers)
    for k, w in order:
        for d in (2, 1, 3):
            i = (k * NH + w) * NX + d
            send(tm.at[i], rm.at[i], s1m.at[i], v1m.at[i], beside[d])
            send(tx.at[i], rx.at[i], s1.at[i], v1.at[i], beside[d])
    for k, w in order:
        j = k * NH + w
        total = part_ref[w, x, k]
        for d in (1, 3, 2):
            i = j * NX + d
            arrived(rm.at[i], s1m.at[i], v1m.at[i])
            arrived(rx.at[i], s1.at[i], v1.at[i])
            total = total + unpack(rx, rm, i)
        pack(total, hs, hm, j)
        send(hm.at[j], hn.at[j], s2m.at[j], v2m.at[j], across)
        send(hs.at[j], hr.at[j], s2.at[j], v2.at[j], across)
    for k, w in order:
        j = k * NH + w
        arrived(hn.at[j], s2m.at[j], v2m.at[j])
        arrived(hr.at[j], s2.at[j], v2.at[j])
        all_ref[w, x, k] = (unpack(hs, hm, j) + unpack(hr, hn, j)).astype(BF16)
        spot = all_ref.at[w, x, k]
        for d in (2, 1, 3):
            i = j * NX + d
            send(spot, spot, s3.at[i], v3.at[i], beside[d])
    for k, w in order:
        for d in (1, 3, 2):
            i = (k * NH + w) * NX + d
            arrived(all_ref.at[w, (x + NX - d) % NX, k], s3.at[i], v3.at[i])
    for copy in sent:
        copy.wait_send()


def scatter_kernel(
    plan_ref, tiles_ref, y_ref, out_ref, own_ref, sums, part_ref, rcore, acc, ty, tym, ryy, rym, tz, tzm, rzz, rzm,
    sc, vc, sy, vy, sym, vym, sz, vz, szm, vzm,
):
    z, y, c = blk_position()
    r = lax.axis_index("rows")
    call(blk_peers(z, y, c, r))
    for k in range(own_ref.shape[0]):
        own_ref[k] = y_ref[r * own_ref.shape[0] + k]
    running_sums(plan_ref, 5, tiles_ref, y_ref, sums, True)
    rows = part_ref.shape[3]
    per = LANES // rows
    for i in range(NZ * NY * NC // per):
        block = block_sum(plan_ref, 5, sums, i)
        for k in range(per):
            j = i * per + k
            part_ref[j // (NY * NC), j // NC % NY, j % NC] = block[k * rows : (k + 1) * rows]
    listen(blk_peers(z, y, c, r))
    partner = (blk_of(z, y, 1 - c), r)
    sent = []

    def send(src, dst, s, v, peer):
        copy = remote(src, dst, s, v, peer)
        copy.start()
        sent.append(copy)

    def arrived(spot, s, v):
        remote(spot, spot, s, v, partner).wait_recv()

    order = (4, 3, 5, 2, 6, 1, 7, 0)
    for d in order:
        send(part_ref.at[(z + d) % NZ, :, 1 - c], rcore.at[d], sc.at[d], vc.at[d], partner)
    for d in order:
        to = (z + d) % NZ
        arrived(rcore.at[d], sc.at[d], vc.at[d])
        for e in (2, 1, 3, 0):
            k = d * NY + e
            ye = (y + e) % NY
            total = part_ref[to, ye, c] + rcore[d, ye]
            if e:
                peer = (blk_of(z, ye, c), r)
                pack(total, ty, tym, k)
                send(tym.at[k], rym.at[k], sym.at[k], vym.at[k], peer)
                send(ty.at[k], ryy.at[k], sy.at[k], vy.at[k], peer)
            else:
                acc[d] = total
    for d in order:
        total = acc[d]
        for e in (1, 3, 2):
            k = d * NY + e
            arrived(rym.at[k], sym.at[k], vym.at[k])
            arrived(ryy.at[k], sy.at[k], vy.at[k])
            total = total + unpack(ryy, rym, k)
        if d:
            peer = (blk_of((z + d) % NZ, y, c), r)
            pack(total, tz, tzm, d)
            send(tzm.at[d], rzm.at[d], szm.at[d], vzm.at[d], peer)
            send(tz.at[d], rzz.at[d], sz.at[d], vz.at[d], peer)
    for d in (1, 7, 2, 6, 3, 5, 4):
        arrived(rzm.at[d], szm.at[d], vzm.at[d])
        arrived(rzz.at[d], sz.at[d], vz.at[d])
        total = total + unpack(rzz, rzm, d)
    out_ref[...] = total
    for copy in sent:
        copy.wait_send()


def vmem(n):
    return [pl.BlockSpec(memory_space=pltpu.VMEM)] * n


def talk(kernel, cid, outs, scratch, *args):
    single = not isinstance(outs, tuple)
    cost = pl.CostEstimate(flops=0, bytes_accessed=64 << 20, transcendentals=0)
    return pl.pallas_call(
        kernel,
        out_shape=outs,
        in_specs=[pl.BlockSpec(memory_space=pltpu.SMEM)] + vmem(len(args) - 1),
        out_specs=vmem(1)[0] if single else tuple(vmem(len(outs))),
        scratch_shapes=scratch,
        cost_estimate=cost,
        compiler_params=pltpu.CompilerParams(
            collective_id=cid, has_side_effects=True, vmem_limit_bytes=32 << 20
        ),
    )(*args)


def dma(*shape):
    return pltpu.SemaphoreType.DMA(shape)


def shards(q_panel, tiles, tile_rows, tile_cols, tile_count, owner_map):
    own_q, rank = q_panel.shape[1:]
    tile_stack = tiles[0, 0]
    size = tile_stack.shape[1]
    blocks = owner_map.shape[1]
    copies = NZ * NY
    listed = jnp.stack(
        [
            jnp.pad(a, (0, LANES - a.shape[0]))
            for a in (tile_rows[0, 0], tile_cols[0, 0, :, 0], owner_map[0])
        ]
        + [jnp.broadcast_to(tile_count[0], (LANES,))]
    ).astype(F32)
    q_all, tile_stack, plan = pl.pallas_call(
        gather_kernel,
        out_shape=(
            jax.ShapeDtypeStruct((NZ, NY, NC, own_q, rank), q_panel.dtype),
            jax.ShapeDtypeStruct(tile_stack.shape, tile_stack.dtype),
            jax.ShapeDtypeStruct((10, LANES), jnp.int32),
        ),
        in_specs=vmem(1) + [pl.BlockSpec(memory_space=pltpu.HBM)] + vmem(1),
        out_specs=tuple(vmem(3)),
        scratch_shapes=[dma(2)] + [dma(NZ)] * 2 + [dma(copies)] * 4,
        compiler_params=pltpu.CompilerParams(
            collective_id=0, has_side_effects=True, vmem_limit_bytes=GRANT
        ),
    )(q_panel[0], tile_stack, listed)
    ncol = NZ * NY * NC * own_q // size
    owned = blocks * size // (NH * NX)
    piece = owned // CH

    def sixteen(n, rows):
        return [pltpu.VMEM((n, rows, rank), jnp.int16), pltpu.VMEM((n, 1, rank), F32)]

    each = NH * CH
    pieces = each * NX
    y_all = talk(
        exchange_kernel, 1,
        jax.ShapeDtypeStruct((NH, NX, CH, piece, rank), BF16),
        [
            pltpu.VMEM((tile_stack.shape[0], size, rank), F32),
            pltpu.VMEM((NH, NX, CH, piece, rank), F32),
        ]
        + sixteen(pieces, piece) * 2 + sixteen(each, piece) * 2
        + [dma(pieces)] * 4 + [dma(each)] * 4 + [dma(pieces)] * 2,
        plan, tile_stack, q_all.reshape(ncol, size, rank),
    )
    z_own, y_own = talk(
        scatter_kernel, 2,
        (
            jax.ShapeDtypeStruct((own_q, rank), F32),
            jax.ShapeDtypeStruct((owned // size, size, rank), BF16),
        ),
        [
            pltpu.VMEM((tile_stack.shape[0], size, rank), F32),
            pltpu.VMEM((NZ, NY, NC, own_q, rank), F32),
            pltpu.VMEM((NZ, NY, own_q, rank), F32),
            pltpu.VMEM((NZ, own_q, rank), F32),
        ]
        + sixteen(copies, own_q) * 2 + sixteen(NZ, own_q) * 2
        + [dma(NZ)] * 2 + [dma(copies)] * 4 + [dma(NZ)] * 4,
        plan, tile_stack, y_all.reshape(blocks, size, rank),
    )
    return (y_own.reshape(1, owned, rank), z_own[None])


def solution(mesh):
    placed = (
        P("rows", "blk", None),
        P("blk", "rows", None, None, None),
        P("blk", "rows", None),
        P("blk", "rows", None, None),
        P("blk", "rows"),
        P("blk", None),
    )
    return jax.shard_map(
        shards,
        mesh=mesh,
        in_specs=placed,
        out_specs=(P("blk", "rows", None), P("rows", "blk", None)),
        check_vma=False,
    )
```

```python
import jax
import jax.numpy as jnp
from jax import lax
from jax.experimental import pallas as pl
from jax.experimental.pallas import tpu as pltpu
from jax.sharding import PartitionSpec as P

MESH = pl.DeviceIdType.MESH
NZ, NY, NC = 8, 4, 2
NH, NX = 2, 4
CH = 4
GROUP = 4
STEPS = 32766.0
TINY = 1e-30
LANES = 128
GRANT = 49 << 20
F32 = jnp.float32
BF16 = jnp.bfloat16


def blk_of(z, y, c):
    return (z * NY + y) * NC + c


def blk_position():
    b = lax.axis_index("blk")
    return b // (NY * NC), (b // NC) % NY, b % NC


def call(peers):
    for peer in peers:
        pl.semaphore_signal(
            pltpu.get_barrier_semaphore(), inc=1, device_id=peer, device_id_type=MESH
        )


def listen(peers):
    pl.semaphore_wait(pltpu.get_barrier_semaphore(), len(peers))


def remote(src, dst, send, recv, peer):
    return pltpu.make_async_remote_copy(
        src_ref=src, dst_ref=dst, send_sem=send, recv_sem=recv, device_id=peer, device_id_type=MESH
    )


def blk_peers(z, y, c, r):
    return (
        [(blk_of((z + d) % NZ, y, c), r) for d in range(1, NZ)]
        + [(blk_of(z, (y + e) % NY, c), r) for e in range(1, NY)]
        + [(blk_of(z, y, 1 - c), r)]
    )


def pack(piece, whole_ref, scale_ref, i):
    top = jnp.maximum(jnp.max(jnp.abs(piece), axis=0, keepdims=True), TINY)
    scale_ref[i] = top * (1.0 / STEPS)
    whole_ref[i] = jnp.round(piece * (STEPS / top)).astype(jnp.int32).astype(jnp.int16)


def unpack(whole_ref, scale_ref, i):
    return whole_ref[i].astype(jnp.int32).astype(F32) * scale_ref[i]


def down(row):
    return jnp.broadcast_to(row, (LANES, LANES)).T


def make_plan(listed_ref, plan_ref):
    lane = lax.broadcasted_iota(jnp.int32, (LANES, LANES), 1).astype(F32)
    deep = lax.broadcasted_iota(jnp.int32, (LANES, LANES), 0).astype(F32)
    rows, cols, owner, count = [listed_ref[i : i + 1, :] for i in range(4)]

    def total(mask, value):
        return jnp.sum(jnp.where(mask, value, 0.0), axis=0, keepdims=True)

    slots = total(deep == rows, down(owner))
    live = lane[0:1] < count
    for at, (mine, other) in enumerate(((slots, cols), (cols, slots))):
        block = jnp.where(live, mine, 1.0 * LANES)
        key = block * LANES + lane[0:1]
        place = total(down(key) < key, 1.0)
        here = down(place) == lane
        before = down(place) == lane - 1.0
        block_down = down(block)
        sorted_block = total(here, block_down)
        keep = jnp.where(total(before, block_down) == sorted_block, 1.0, 0.0)
        keep = jnp.where(lane[0:1] == 0.0, 0.0, keep)
        last = jnp.maximum(total(block_down <= lane, 1.0) - 1.0, 0.0)
        has = jnp.where(total(block_down == lane, 1.0) > 0.0, 1.0, 0.0)
        for i, row in enumerate((total(here, deep), keep, total(here, down(other)), last, has)):
            plan_ref[5 * at + i : 5 * at + i + 1, :] = row.astype(jnp.int32)


def running_sums(plan_ref, first, tiles_ref, from_ref, sums, turned):
    across = (((0,), (0,)), ((), ())) if turned else (((1,), (0,)), ((), ()))

    def step(p, total):
        term = lax.dot_general(
            tiles_ref[plan_ref[first, p]], from_ref[plan_ref[first + 2, p]], across,
            preferred_element_type=F32,
        )
        total = total * plan_ref[first + 1, p].astype(F32) + term
        sums[p] = total
        return total

    start = jnp.zeros(sums.shape[1:], F32)
    lax.fori_loop(0, tiles_ref.shape[0], step, start, unroll=4)


def block_sum(plan_ref, first, sums, i):
    return sums[plan_ref[first + 3, i]] * plan_ref[first + 4, i].astype(F32)


def gather_kernel(q_ref, held_ref, listed_ref, out_ref, moved_ref, plan_ref, lsem, sz, rz, sy, ry, sc, rc):
    z, y, c = blk_position()
    r = lax.axis_index("rows")
    call(blk_peers(z, y, c, r))
    local = pltpu.make_async_copy(held_ref, moved_ref, lsem.at[1])
    local.start()
    make_plan(listed_ref, plan_ref)
    listen(blk_peers(z, y, c, r))
    partner = (blk_of(z, y, 1 - c), r)
    own = pltpu.make_async_copy(q_ref, out_ref.at[z, y, c], lsem.at[0])
    own.start()
    sent = []

    def send(src, dst, s, v, peer):
        copy = remote(src, dst, s, v, peer)
        copy.start()
        sent.append(copy)

    for d in (4, 3, 5, 2, 6, 1, 7):
        send(q_ref, out_ref.at[z, y, c], sz.at[d], rz.at[d], (blk_of((z + d) % NZ, y, c), r))
    order = (0, 1, 7, 2, 6, 3, 5, 4)
    for d in order:
        zs = (z + NZ - d) % NZ
        spot = out_ref.at[zs, y, c]
        src = q_ref if d == 0 else spot
        if d:
            remote(spot, spot, sz.at[d], rz.at[d], partner).wait_recv()
        for e in (2, 1, 3):
            send(src, spot, sy.at[d * NY + e], ry.at[d * NY + e], (blk_of(z, (y + e) % NY, c), r))
        send(src, spot, sc.at[d * NY], rc.at[d * NY], partner)
    for d in order:
        zs = (z + NZ - d) % NZ
        for e in (1, 3, 2):
            k = d * NY + e
            spot = out_ref.at[zs, (y + NY - e) % NY, c]
            remote(spot, spot, sy.at[k], ry.at[k], partner).wait_recv()
            send(spot, spot, sc.at[k], rc.at[k], partner)
    for d in order:
        zs = (z + NZ - d) % NZ
        for e in range(NY):
            k = d * NY + e
            spot = out_ref.at[zs, (y + NY - e) % NY, 1 - c]
            remote(spot, spot, sc.at[k], rc.at[k], partner).wait_recv()
    own.wait()
    local.wait()
    for copy in sent:
        copy.wait_send()


def exchange_kernel(
    plan_ref, tiles_ref, q_ref, all_ref, sums, tx, tm, rx, rm, hs, hm, hr, hn,
    s1, v1, s1m, v1m, s2, v2, s2m, v2m, s3, v3,
):
    b = lax.axis_index("blk")
    r = lax.axis_index("rows")
    h, x = r // NX, r % NX
    across = (b, (1 - h) * NX + x)
    beside = [None] + [(b, h * NX + (x + d) % NX) for d in range(1, NX)]
    peers = beside[1:] + [across]
    call(peers)
    piece = all_ref.shape[3]
    order = [(k, w) for k in range(CH) for w in range(NH)]
    sent = []

    def send(src, dst, s, v, peer):
        copy = remote(src, dst, s, v, peer)
        copy.start()
        sent.append(copy)

    def arrived(spot, s, v):
        remote(spot, spot, s, v, across).wait_recv()

    running_sums(plan_ref, 0, tiles_ref, q_ref, sums, False)
    listen(peers)

    def own_piece(w, to, k):
        i = ((w * NX + to) * CH + k) * piece // LANES
        low = k * piece % LANES
        return sums[plan_ref[3, i], low : low + piece] * plan_ref[4, i].astype(F32)

    for k, w in order:
        for d in (2, 1, 3):
            i = (k * NH + w) * NX + d
            pack(own_piece(w, (x + d) % NX, k), tx, tm, i)
            send(tm.at[i], rm.at[i], s1m.at[i], v1m.at[i], beside[d])
            send(tx.at[i], rx.at[i], s1.at[i], v1.at[i], beside[d])
    for k, w in order:
        j = k * NH + w
        total = own_piece(w, x, k)
        for d in (1, 3, 2):
            i = j * NX + d
            arrived(rm.at[i], s1m.at[i], v1m.at[i])
            arrived(rx.at[i], s1.at[i], v1.at[i])
            total = total + unpack(rx, rm, i)
        pack(total, hs, hm, j)
        send(hm.at[j], hn.at[j], s2m.at[j], v2m.at[j], across)
        send(hs.at[j], hr.at[j], s2.at[j], v2.at[j], across)
    for k, w in order:
        j = k * NH + w
        arrived(hn.at[j], s2m.at[j], v2m.at[j])
        arrived(hr.at[j], s2.at[j], v2.at[j])
        all_ref[w, x, k] = (unpack(hs, hm, j) + unpack(hr, hn, j)).astype(BF16)
        spot = all_ref.at[w, x, k]
        for d in (2, 1, 3):
            i = j * NX + d
            send(spot, spot, s3.at[i], v3.at[i], beside[d])
    for k, w in order:
        for d in (1, 3, 2):
            i = (k * NH + w) * NX + d
            arrived(all_ref.at[w, (x + NX - d) % NX, k], s3.at[i], v3.at[i])
    for copy in sent:
        copy.wait_send()


def scatter_kernel(
    plan_ref, tiles_ref, y_ref, out_ref, own_ref, sums, part_ref, rcore, acc, ty, tym, ryy, rym, tz, tzm, rzz, rzm,
    sc, vc, sy, vy, sym, vym, sz, vz, szm, vzm,
):
    z, y, c = blk_position()
    r = lax.axis_index("rows")
    call(blk_peers(z, y, c, r))
    for k in range(own_ref.shape[0]):
        own_ref[k] = y_ref[r * own_ref.shape[0] + k]
    running_sums(plan_ref, 5, tiles_ref, y_ref, sums, True)
    rows = part_ref.shape[3]
    per = LANES // rows
    listen(blk_peers(z, y, c, r))
    partner = (blk_of(z, y, 1 - c), r)
    sent = []

    def send(src, dst, s, v, peer):
        copy = remote(src, dst, s, v, peer)
        copy.start()
        sent.append(copy)

    def arrived(spot, s, v):
        remote(spot, spot, s, v, partner).wait_recv()

    order = (4, 3, 5, 2, 6, 1, 7, 0)
    for d in order:
        to = (z + d) % NZ
        for i in range(NY * NC // per):
            block = block_sum(plan_ref, 5, sums, to * (NY * NC // per) + i)
            for k in range(per):
                j = i * per + k
                part_ref[to, j // NC, j % NC] = block[k * rows : (k + 1) * rows]
        send(part_ref.at[to, :, 1 - c], rcore.at[d], sc.at[d], vc.at[d], partner)
    for d in order:
        to = (z + d) % NZ
        arrived(rcore.at[d], sc.at[d], vc.at[d])
        for e in (2, 1, 3, 0):
            k = d * NY + e
            ye = (y + e) % NY
            total = part_ref[to, ye, c] + rcore[d, ye]
            if e:
                peer = (blk_of(z, ye, c), r)
                pack(total, ty, tym, k)
                send(tym.at[k], rym.at[k], sym.at[k], vym.at[k], peer)
                send(ty.at[k], ryy.at[k], sy.at[k], vy.at[k], peer)
            else:
                acc[d] = total
    for d in order:
        total = acc[d]
        for e in (1, 3, 2):
            k = d * NY + e
            arrived(rym.at[k], sym.at[k], vym.at[k])
            arrived(ryy.at[k], sy.at[k], vy.at[k])
            total = total + unpack(ryy, rym, k)
        if d:
            peer = (blk_of((z + d) % NZ, y, c), r)
            pack(total, tz, tzm, d)
            send(tzm.at[d], rzm.at[d], szm.at[d], vzm.at[d], peer)
            send(tz.at[d], rzz.at[d], sz.at[d], vz.at[d], peer)
    for d in (1, 7, 2, 6, 3, 5, 4):
        arrived(rzm.at[d], szm.at[d], vzm.at[d])
        arrived(rzz.at[d], sz.at[d], vz.at[d])
        total = total + unpack(rzz, rzm, d)
    out_ref[...] = total
    for copy in sent:
        copy.wait_send()


def vmem(n):
    return [pl.BlockSpec(memory_space=pltpu.VMEM)] * n


def talk(kernel, cid, outs, scratch, *args):
    single = not isinstance(outs, tuple)
    cost = pl.CostEstimate(flops=0, bytes_accessed=64 << 20, transcendentals=0)
    return pl.pallas_call(
        kernel,
        out_shape=outs,
        in_specs=[pl.BlockSpec(memory_space=pltpu.SMEM)] + vmem(len(args) - 1),
        out_specs=vmem(1)[0] if single else tuple(vmem(len(outs))),
        scratch_shapes=scratch,
        cost_estimate=cost,
        compiler_params=pltpu.CompilerParams(
            collective_id=cid, has_side_effects=True, vmem_limit_bytes=32 << 20
        ),
    )(*args)


def dma(*shape):
    return pltpu.SemaphoreType.DMA(shape)


def shards(q_panel, tiles, tile_rows, tile_cols, tile_count, owner_map):
    own_q, rank = q_panel.shape[1:]
    tile_stack = tiles[0, 0]
    size = tile_stack.shape[1]
    blocks = owner_map.shape[1]
    copies = NZ * NY
    listed = jnp.stack(
        [
            jnp.pad(a, (0, LANES - a.shape[0]))
            for a in (tile_rows[0, 0], tile_cols[0, 0, :, 0], owner_map[0])
        ]
        + [jnp.broadcast_to(tile_count[0], (LANES,))]
    ).astype(F32)
    q_all, tile_stack, plan = pl.pallas_call(
        gather_kernel,
        out_shape=(
            jax.ShapeDtypeStruct((NZ, NY, NC, own_q, rank), q_panel.dtype),
            jax.ShapeDtypeStruct(tile_stack.shape, tile_stack.dtype),
            jax.ShapeDtypeStruct((10, LANES), jnp.int32),
        ),
        in_specs=vmem(1) + [pl.BlockSpec(memory_space=pltpu.HBM)] + vmem(1),
        out_specs=tuple(vmem(3)),
        scratch_shapes=[dma(2)] + [dma(NZ)] * 2 + [dma(copies)] * 4,
        compiler_params=pltpu.CompilerParams(
            collective_id=0, has_side_effects=True, vmem_limit_bytes=GRANT
        ),
    )(q_panel[0], tile_stack, listed)
    ncol = NZ * NY * NC * own_q // size
    owned = blocks * size // (NH * NX)
    piece = owned // CH

    def sixteen(n, rows):
        return [pltpu.VMEM((n, rows, rank), jnp.int16), pltpu.VMEM((n, 1, rank), F32)]

    each = NH * CH
    pieces = each * NX
    y_all = talk(
        exchange_kernel, 1,
        jax.ShapeDtypeStruct((NH, NX, CH, piece, rank), BF16),
        [
            pltpu.VMEM((tile_stack.shape[0], size, rank), F32),
        ]
        + sixteen(pieces, piece) * 2 + sixteen(each, piece) * 2
        + [dma(pieces)] * 4 + [dma(each)] * 4 + [dma(pieces)] * 2,
        plan, tile_stack, q_all.reshape(ncol, size, rank),
    )
    z_own, y_own = talk(
        scatter_kernel, 2,
        (
            jax.ShapeDtypeStruct((own_q, rank), F32),
            jax.ShapeDtypeStruct((owned // size, size, rank), BF16),
        ),
        [
            pltpu.VMEM((tile_stack.shape[0], size, rank), F32),
            pltpu.VMEM((NZ, NY, NC, own_q, rank), F32),
            pltpu.VMEM((NZ, NY, own_q, rank), F32),
            pltpu.VMEM((NZ, own_q, rank), F32),
        ]
        + sixteen(copies, own_q) * 2 + sixteen(NZ, own_q) * 2
        + [dma(NZ)] * 2 + [dma(copies)] * 4 + [dma(NZ)] * 4,
        plan, tile_stack, y_all.reshape(blocks, size, rank),
    )
    return (y_own.reshape(1, owned, rank), z_own[None])


def solution(mesh):
    placed = (
        P("rows", "blk", None),
        P("blk", "rows", None, None, None),
        P("blk", "rows", None),
        P("blk", "rows", None, None),
        P("blk", "rows"),
        P("blk", None),
    )
    return jax.shard_map(
        shards,
        mesh=mesh,
        in_specs=placed,
        out_specs=(P("blk", "rows", None), P("rows", "blk", None)),
        check_vma=False,
    )
```
